32 devices in a mesh: energy: 16 (over z, y, x), space: 2 (over core).
Axes of the slice: x: 2, y: 2, z: 4, core: 2. Of those that a mesh axis runs over, the one named last changes fastest.
Arguments:
- lesser: bfloat16 [32, 2, 2, 256, 256], P('energy', 'space'), may hold values from -6 to 6
- greater: bfloat16 [32, 2, 2, 256, 256], P('energy', 'space'), may hold values from -6 to 6
- coulomb_diag: bfloat16 [2, 256, 256], P('space'), may hold values from -0.375 to 0.375
- coulomb_upper: bfloat16 [2, 256, 256], P('space'), may hold values from -0.375 to 0.375
Outputs:
- screened: bfloat16 [32, 2, 2, 256, 256], P('energy', 'space')
The draws below stay inside these ranges and needn't reach their ends.
All inputs are finite; a program needn't handle non-finite values.
Results may differ from the reference program's by a relative error of at most 0.015.
Values may be sent and summed in bfloat16 or wider, within the bound.
A program may use at most 64 MiB of HBM per device.

```python
import jax
import jax.numpy as jnp
from jax import lax

BS = 256
NE = 32
NB = 2


def shard_levels(stream_key, extent, shards, low, largest):
    def one(axis_at, shards_of):
        heights = jax.random.uniform(jax.random.fold_in(jax.random.fold_in(stream_key, 6), axis_at), (shards_of,), jnp.float32, low / len(shards), largest / len(shards))
        return jnp.repeat(jnp.exp(heights), extent[axis_at] // shards_of).reshape((-1,) + (1,) * (len(extent) - axis_at - 1))

    level = one(*shards[0])
    for cut in shards[1:]:
        level = level * one(*cut)
    return level


def normal_values(rng, shape, scale, limit, cuts=(), dtype=jnp.bfloat16):
    entries = scale * jax.random.normal(rng, shape, jnp.float32)
    if cuts:
        entries = entries * shard_levels(rng, shape, cuts, -0.22, 0.18)
    return jnp.clip(entries, -limit, limit).astype(dtype)


def setup_inputs(seed: int = 0) -> dict:
    arg_keys = jax.random.split(jax.random.key(seed), 5)
    return {
        "lesser": normal_values(arg_keys[0], (NE, NB, 2, BS, BS), 1.0, 6.0, ((0, 16), (1, 2))),
        "greater": normal_values(arg_keys[1], (NE, NB, 2, BS, BS), 1.0, 6.0, ((0, 16), (1, 2))),
        "coulomb_diag": normal_values(arg_keys[2], (NB, BS, BS), BS ** -0.5, 0.375, ((0, 2),)),
        "coulomb_upper": normal_values(arg_keys[3], (NB, BS, BS), BS ** -0.5, 0.375, ((0, 2),)),
    }


def widen(values):
    return values.astype(jnp.float32)


def polar_row(lesser_row, greater_row):
    length = 2 * NE
    lesser_re = widen(lesser_row[:, 0])
    lesser_im = widen(lesser_row[:, 1])
    greater_re = widen(greater_row[:, 0])
    greater_im = widen(greater_row[:, 1])

    def forward(values):
        return jnp.fft.rfft(values, n=length, axis=0)

    def reverse(values):
        return jnp.fft.rfft(values[::-1], n=length, axis=0)

    def inverse(values):
        return jnp.fft.irfft(values, n=length, axis=0)[NE - 1:2 * NE - 1]

    spec_lre = forward(lesser_re)
    spec_lim = forward(lesser_im)
    spec_gre = reverse(greater_re)
    spec_gim = reverse(greater_im)
    corr_re = inverse(spec_lre * spec_gre - spec_lim * spec_gim).astype(jnp.float32)
    corr_im = inverse(spec_lre * spec_gim + spec_lim * spec_gre).astype(jnp.float32)
    factor = jnp.float32(NE) ** -0.5
    return jnp.stack([corr_im * factor, -corr_re * factor], axis=1).astype(jnp.bfloat16)


def reference(lesser, greater, coulomb_diag, coulomb_upper):
    greater_t = jnp.swapaxes(greater, 3, 4)

    def one_row(pair):
        return polar_row(pair[0], pair[1])

    polar = lax.map(one_row, (jnp.moveaxis(lesser, 1, 0), jnp.moveaxis(greater_t, 1, 0)))
    polar = jnp.moveaxis(polar, 0, 1)
    zero_row = jnp.zeros_like(polar[:, :1])
    polar_next = jnp.concatenate([polar[:, 1:], zero_row], axis=1)
    polar_prev = jnp.concatenate([zero_row, polar[:, :-1]], axis=1)
    upper_prev = jnp.concatenate([jnp.zeros_like(coulomb_upper[:1]), coulomb_upper[:-1]], axis=0)

    def screen(blocks):
        own, after, before = blocks
        left = jnp.einsum('iab,icbd->icad', widen(coulomb_diag), widen(own)).astype(jnp.bfloat16)
        total = jnp.einsum('icad,ifd->icaf', widen(left), widen(coulomb_diag))
        left = jnp.einsum('iab,icbd->icad', widen(coulomb_upper), widen(after)).astype(jnp.bfloat16)
        total = total + jnp.einsum('icad,ifd->icaf', widen(left), widen(coulomb_upper))
        left = jnp.einsum('iba,icbd->icad', widen(upper_prev), widen(before)).astype(jnp.bfloat16)
        total = total + jnp.einsum('icad,idf->icaf', widen(left), widen(upper_prev))
        return total.astype(jnp.bfloat16)

    return lax.map(screen, (polar, polar_next, polar_prev))
```

```python
import functools
import math

import jax
import jax.numpy as jnp
from jax import lax
from jax.experimental import pallas as pl
from jax.experimental.pallas import tpu as pltpu
from jax.sharding import PartitionSpec as P


def from_behind(value, axis, steps):
    count = lax.axis_size(axis)
    leading, last = (max(0, -steps), min(count, count - steps))
    return lax.ppermute(value, axis, [(source, source + steps) for source in range(leading, last)])


def split_parts(values):
    high = values.astype(jnp.bfloat16)
    low = (values - high.astype(jnp.float32)).astype(jnp.bfloat16)
    return (high, low)


def product_two(table, data_bf):
    return jnp.dot(table[0], data_bf, preferred_element_type=jnp.float32) + jnp.dot(
        table[1], data_bf, preferred_element_type=jnp.float32
    )


def product_three(table, data_f32):
    data_high, data_low = split_parts(data_f32)
    total = jnp.dot(table[0], data_high, preferred_element_type=jnp.float32)
    total = total + jnp.dot(table[1], data_high, preferred_element_type=jnp.float32)
    return total + jnp.dot(table[0], data_low, preferred_element_type=jnp.float32)


def correlate(lesser_x, greater_x):
    energies = lesser_x.shape[0]
    length = 2 * energies
    tail_shape = lesser_x.shape[1:]

    def flatten(values, part):
        return values[:, :, part].reshape(energies, -1)

    lesser_re = flatten(lesser_x, 0)
    lesser_im = flatten(lesser_x, 1)
    greater_re = flatten(greater_x, 0)
    greater_im = flatten(greater_x, 1)
    freqs = lax.broadcasted_iota(jnp.int32, (length, energies), 0)
    places = lax.broadcasted_iota(jnp.int32, (length, energies), 1)
    angles = 2.0 * math.pi / length * jnp.mod(freqs * places, length).astype(jnp.float32)
    cosine = split_parts(jnp.cos(angles))
    sine = split_parts(jnp.sin(angles))
    cosine_t = split_parts(jnp.cos(angles).T)
    sine_t = split_parts(jnp.sin(angles).T)
    hat_lre = product_two(cosine, lesser_re) + product_two(sine, lesser_im)
    hat_lim = product_two(cosine, lesser_im) - product_two(sine, lesser_re)
    hat_gre = product_two(cosine, greater_re) - product_two(sine, greater_im)
    hat_gim = product_two(cosine, greater_im) + product_two(sine, greater_re)
    prod_re = hat_lre * hat_gre - hat_lim * hat_gim
    prod_im = hat_lre * hat_gim + hat_lim * hat_gre
    corr_re = (product_three(cosine_t, prod_re) - product_three(sine_t, prod_im)) / length
    corr_im = (product_three(cosine_t, prod_im) + product_three(sine_t, prod_re)) / length
    factor = jnp.float32(energies) ** (-0.5)
    shaped = (energies, tail_shape[0], tail_shape[2], tail_shape[3])
    real_part = (corr_im * factor).reshape(shaped)
    imag_part = (-corr_re * factor).reshape(shaped)
    return jnp.stack([real_part, imag_part], axis=2).astype(jnp.bfloat16)


def left_plain(coupler, blocks):
    return jnp.einsum("ab,ecbd->ecad", coupler, blocks, preferred_element_type=jnp.float32).astype(
        jnp.bfloat16
    )


def left_transposed(coupler, blocks):
    return jnp.einsum("ba,ecbd->ecad", coupler, blocks, preferred_element_type=jnp.float32).astype(
        jnp.bfloat16
    )


def right_transposed(left, coupler):
    return jnp.einsum("ecad,fd->ecaf", left, coupler, preferred_element_type=jnp.float32)


def right_plain(left, coupler):
    return jnp.einsum("ecad,df->ecaf", left, coupler, preferred_element_type=jnp.float32)


def per_device(lesser, greater, coulomb_diag, coulomb_upper):
    greater_t = jnp.swapaxes(greater, 3, 4)
    lesser_x, greater_x = (
        lax.all_to_all(lesser, "energy", split_axis=3, concat_axis=0, tiled=True),
        lax.all_to_all(greater_t, "energy", split_axis=3, concat_axis=0, tiled=True),
    )
    polar_x = correlate(lesser_x, greater_x)
    polar = lax.all_to_all(polar_x, "energy", split_axis=0, concat_axis=3, tiled=True)
    own = polar[:, 0]
    diag_block = coulomb_diag[0]
    upper_block = coulomb_upper[0]
    total = right_transposed(left_plain(diag_block, own), diag_block)
    polar_next = from_behind(polar, "space", -1)
    outgoing = right_plain(left_transposed(upper_block, own), upper_block)
    total = total + right_transposed(left_plain(upper_block, polar_next[:, 0]), upper_block)
    incoming = from_behind(outgoing.astype(jnp.bfloat16), "space", 1).astype(outgoing.dtype)
    total = total + incoming
    return total.astype(jnp.bfloat16)[:, None]


LAGS = 8
STEPS = 4
LANES = 128
MESH = pl.DeviceIdType.MESH


def to_energy(dest):
    return {"energy": dest}


def correlate_chunk(chunk, energies, lx, hx, lf, hf, cf, cx):
    rows = lf.shape[2]
    flat = (energies, rows, LANES)
    for part_of, held in ((lx, lf), (hx, hf)):
        re = part_of[chunk, :, :, 0].reshape(flat).astype(jnp.float32)
        im = part_of[chunk, :, :, 1].reshape(flat).astype(jnp.float32)
        held[0, pl.ds(0, energies)] = re
        held[1, pl.ds(0, energies)] = im
        held[2, pl.ds(0, energies)] = re + im
    factor = float(energies) ** -0.5

    def one_slab(slab, carry):
        at = pl.ds(pl.multiple_of(slab * 8, 8), 8)
        for first in range(0, energies, LAGS):
            def step(turn, sums):
                start = turn * STEPS
                sums = list(sums)
                for q in range(3):
                    window = [lf[q, start + (first + t), at, :] for t in range(LAGS + STEPS - 1)]
                    taps = [hf[q, start + u, at, :] for u in range(STEPS)]
                    for u in range(STEPS):
                        for j in range(LAGS):
                            sums[q * LAGS + j] = sums[q * LAGS + j] + window[j + u] * taps[u]
                return tuple(sums)

            zero = jnp.zeros((8, LANES), jnp.float32)
            sums = lax.fori_loop(0, (energies - first) // STEPS, step, (zero,) * (3 * LAGS))
            for j in range(LAGS):
                rr, ii, mixed = sums[j], sums[LAGS + j], sums[2 * LAGS + j]
                cf[first + j, 0, at, :] = (mixed - rr - ii) * factor
                cf[first + j, 1, at, :] = (ii - rr) * factor
        return carry

    lax.fori_loop(0, rows // 8, one_slab, 0)
    cx[chunk] = cf[...].astype(jnp.bfloat16).reshape(cx.shape[1:])


def kernel(
    n, ns, lesser, greater, diag, upper, out,
    gv, ht, lx, hx, lf, hf, cf, cx, polar, side, uprev, wside, total,
    local_sem, send_sem, recv_l, recv_h, recv_p, side_send, side_recv, u_send, u_recv,
):
    me = lax.axis_index("energy")
    row = lax.axis_index("space")
    chunks, _, k, _, rows, _ = lx.shape
    energies = n * k
    has_next = row < ns - 1
    has_prev = row > 0

    barrier = pltpu.get_barrier_semaphore()

    def greet(step, carry):
        pl.semaphore_signal(
            barrier, inc=1, device_id=to_energy(lax.rem(me + step, n)), device_id_type=MESH
        )
        return carry

    lax.fori_loop(1, n, greet, 0)

    @pl.when(has_next)
    def _():
        pl.semaphore_signal(barrier, inc=1, device_id={"space": row + 1}, device_id_type=MESH)

    @pl.when(has_prev)
    def _():
        pl.semaphore_signal(barrier, inc=1, device_id={"space": row - 1}, device_id_type=MESH)

    load = pltpu.make_async_copy(greater.at[:, 0], gv, local_sem.at[0])
    load.start()

    zeros = jnp.zeros((lf.shape[1] - energies,) + lf.shape[2:], jnp.float32)
    for q in range(3):
        lf[q, pl.ds(energies, lf.shape[1] - energies)] = zeros

    pl.semaphore_wait(
        barrier, n - 1 + has_next.astype(jnp.int32) + has_prev.astype(jnp.int32)
    )

    def scatter(source, held, c, kind, recv):
        cols = pl.ds(c * LANES, LANES)

        def part(dest):
            return source.at[:, :, pl.ds(pl.multiple_of(dest * rows, rows), rows), cols]

        def push(step, carry):
            dest = lax.rem(me + step, n)
            pltpu.make_async_remote_copy(
                src_ref=part(dest), dst_ref=held.at[c, me], send_sem=send_sem.at[kind],
                recv_sem=recv.at[c], device_id=to_energy(dest), device_id_type=MESH,
            ).start()
            return carry

        lax.fori_loop(1, n, push, 0)
        pltpu.make_async_copy(part(me), held.at[c, me], recv.at[c]).start()

    u_copy = pltpu.make_async_remote_copy(
        src_ref=upper.at[0], dst_ref=uprev, send_sem=u_send, recv_sem=u_recv,
        device_id={"space": lax.rem(row + 1, ns)}, device_id_type=MESH,
    )

    @pl.when(has_next)
    def _():
        u_copy.start()

    scatter(lesser.at[:, 0], lx, 0, 0, recv_l)
    load.wait()
    for e in range(k):
        for part_at in range(2):
            ht[e, part_at] = gv[e, part_at].T
    scatter(ht, hx, 0, 1, recv_h)
    for c in range(1, chunks):
        scatter(lesser.at[:, 0], lx, c, 0, recv_l)
        scatter(ht, hx, c, 1, recv_h)

    wside[0] = upper[0]

    @pl.when(has_prev)
    def _():
        u_copy.wait_recv()
        wside[1] = uprev[...].T

    def one_chunk(c, carry):
        pltpu.make_async_copy(lx.at[c], lx.at[c], recv_l.at[c]).wait()
        pltpu.make_async_copy(hx.at[c], hx.at[c], recv_h.at[c]).wait()
        correlate_chunk(c, energies, lx, hx, lf, hf, cf, cx)
        mine = pl.ds(pl.multiple_of(me * rows, rows), rows)

        def push(step, carry_in):
            dest = lax.rem(me + step, n)
            pltpu.make_async_remote_copy(
                src_ref=cx.at[c, dest], dst_ref=polar.at[c, :, :, mine, :],
                send_sem=send_sem.at[2], recv_sem=recv_p.at[c],
                device_id=to_energy(dest), device_id_type=MESH,
            ).start()
            return carry_in

        lax.fori_loop(1, n, push, 0)
        pltpu.make_async_copy(cx.at[c, me], polar.at[c, :, :, mine, :], recv_p.at[c]).start()
        return carry

    lax.fori_loop(0, chunks, one_chunk, 0)

    def screen(block, coupler, slot, c, begin):
        right = coupler[:, c * LANES:(c + 1) * LANES]
        for e in range(k):
            pair = jnp.concatenate([block[slot, e, 0], block[slot, e, 1]], axis=1)
            left = jnp.dot(coupler, pair, preferred_element_type=jnp.float32).astype(jnp.bfloat16)
            for part_at in range(2):
                term = lax.dot_general(
                    left[:, part_at * LANES:(part_at + 1) * LANES], right,
                    (((1,), (1,)), ((), ())), preferred_element_type=jnp.float32,
                )
                if begin:
                    total[e, part_at] = term
                else:
                    total[e, part_at] += term

    def forward(c, slot, to):
        return pltpu.make_async_remote_copy(
            src_ref=polar.at[c], dst_ref=side.at[slot, c], send_sem=side_send.at[slot, c],
            recv_sem=side_recv.at[slot, c], device_id={"space": to}, device_id_type=MESH,
        )

    up, down = lax.rem(row + 1, ns), lax.rem(row + ns - 1, ns)
    for c in range(chunks):
        pltpu.make_async_copy(polar.at[c], polar.at[c], recv_p.at[c]).wait()

        @pl.when(has_prev)
        def _():
            forward(c, 0, down).start()

        @pl.when(has_next)
        def _():
            forward(c, 1, up).start()

        screen(polar, diag[0], c, c, c == 0)

        @pl.when(has_next)
        def _():
            forward(c, 0, down).wait_recv()
            screen(side.at[0], wside[0], c, c, False)

        @pl.when(has_prev)
        def _():
            forward(c, 1, up).wait_recv()
            screen(side.at[1], wside[1], c, c, False)

    out[:, 0] = total[...].astype(jnp.bfloat16)

    for c in range(chunks):
        @pl.when(has_prev)
        def _():
            forward(c, 0, down).wait_send()

        @pl.when(has_next)
        def _():
            forward(c, 1, up).wait_send()

    @pl.when(has_next)
    def _():
        u_copy.wait_send()

    for kind in range(3):
        sent = lx.at[:, pl.ds(0, n - 1)]
        pltpu.make_async_copy(sent, sent, send_sem.at[kind]).wait()


def fused(n, ns, lesser, greater, diag, upper):
    k, _, _, size, _ = lesser.shape
    rows, chunks, energies = size // n, size // LANES, n * k
    bf, f32 = jnp.bfloat16, jnp.float32
    whole = (k, 2, size, size)
    padded = energies + LAGS + STEPS
    dma = pltpu.SemaphoreType.DMA
    vmem = pl.BlockSpec(memory_space=pltpu.VMEM)
    hbm = pl.BlockSpec(memory_space=pl.ANY)
    return pl.pallas_call(
        functools.partial(kernel, n, ns),
        out_shape=jax.ShapeDtypeStruct(lesser.shape, bf),
        in_specs=[hbm, hbm, vmem, vmem],
        out_specs=vmem,
        scratch_shapes=[
            pltpu.VMEM(whole, bf),
            pltpu.VMEM(whole, bf),
            pltpu.VMEM((chunks, n, k, 2, rows, LANES), bf),
            pltpu.VMEM((chunks, n, k, 2, rows, LANES), bf),
            pltpu.VMEM((3, padded, rows, LANES), f32),
            pltpu.VMEM((3, energies, rows, LANES), f32),
            pltpu.VMEM((energies, 2, rows, LANES), f32),
            pltpu.VMEM((chunks, n, k, 2, rows, LANES), bf),
            pltpu.VMEM((chunks, k, 2, size, LANES), bf),
            pltpu.VMEM((2, chunks, k, 2, size, LANES), bf),
            pltpu.VMEM((size, size), bf),
            pltpu.VMEM((2, size, size), bf),
            pltpu.VMEM(whole, f32),
            dma((1,)), dma((3,)), dma((chunks,)), dma((chunks,)), dma((chunks,)),
            dma((2, chunks)), dma((2, chunks)), dma, dma,
        ],
        compiler_params=pltpu.CompilerParams(
            collective_id=0, has_side_effects=True, vmem_limit_bytes=40 << 20
        ),
    )(lesser, greater, diag, upper)


def fits(n, ns, size, energies):
    return size % n == 0 and (size // n) % 16 == 0 and size % LANES == 0 and energies % LAGS == 0 and ns > 1


def either(n, ns, lesser, greater, diag, upper):
    if fits(n, ns, lesser.shape[3], n * lesser.shape[0]):
        return fused(n, ns, lesser, greater, diag, upper)
    return per_device(lesser, greater, diag, upper)


def solution(mesh):
    placed = (
        P("energy", "space", None, None, None),
        P("energy", "space", None, None, None),
        P("space", None, None),
        P("space", None, None),
    )
    return jax.shard_map(
        functools.partial(either, mesh.shape["energy"], mesh.shape["space"]),
        mesh=mesh,
        in_specs=placed,
        out_specs=P("energy", "space", None, None, None),
        check_vma=False,
    )
```

```python
import functools
import math

import jax
import jax.numpy as jnp
from jax import lax
from jax.experimental import pallas as pl
from jax.experimental.pallas import tpu as pltpu
from jax.sharding import PartitionSpec as P


def from_behind(value, axis, steps):
    count = lax.axis_size(axis)
    leading, last = (max(0, -steps), min(count, count - steps))
    return lax.ppermute(value, axis, [(source, source + steps) for source in range(leading, last)])


def split_parts(values):
    high = values.astype(jnp.bfloat16)
    low = (values - high.astype(jnp.float32)).astype(jnp.bfloat16)
    return (high, low)


def product_two(table, data_bf):
    return jnp.dot(table[0], data_bf, preferred_element_type=jnp.float32) + jnp.dot(
        table[1], data_bf, preferred_element_type=jnp.float32
    )


def product_three(table, data_f32):
    data_high, data_low = split_parts(data_f32)
    total = jnp.dot(table[0], data_high, preferred_element_type=jnp.float32)
    total = total + jnp.dot(table[1], data_high, preferred_element_type=jnp.float32)
    return total + jnp.dot(table[0], data_low, preferred_element_type=jnp.float32)


def correlate(lesser_x, greater_x):
    energies = lesser_x.shape[0]
    length = 2 * energies
    tail_shape = lesser_x.shape[1:]

    def flatten(values, part):
        return values[:, :, part].reshape(energies, -1)

    lesser_re = flatten(lesser_x, 0)
    lesser_im = flatten(lesser_x, 1)
    greater_re = flatten(greater_x, 0)
    greater_im = flatten(greater_x, 1)
    freqs = lax.broadcasted_iota(jnp.int32, (length, energies), 0)
    places = lax.broadcasted_iota(jnp.int32, (length, energies), 1)
    angles = 2.0 * math.pi / length * jnp.mod(freqs * places, length).astype(jnp.float32)
    cosine = split_parts(jnp.cos(angles))
    sine = split_parts(jnp.sin(angles))
    cosine_t = split_parts(jnp.cos(angles).T)
    sine_t = split_parts(jnp.sin(angles).T)
    hat_lre = product_two(cosine, lesser_re) + product_two(sine, lesser_im)
    hat_lim = product_two(cosine, lesser_im) - product_two(sine, lesser_re)
    hat_gre = product_two(cosine, greater_re) - product_two(sine, greater_im)
    hat_gim = product_two(cosine, greater_im) + product_two(sine, greater_re)
    prod_re = hat_lre * hat_gre - hat_lim * hat_gim
    prod_im = hat_lre * hat_gim + hat_lim * hat_gre
    corr_re = (product_three(cosine_t, prod_re) - product_three(sine_t, prod_im)) / length
    corr_im = (product_three(cosine_t, prod_im) + product_three(sine_t, prod_re)) / length
    factor = jnp.float32(energies) ** (-0.5)
    shaped = (energies, tail_shape[0], tail_shape[2], tail_shape[3])
    real_part = (corr_im * factor).reshape(shaped)
    imag_part = (-corr_re * factor).reshape(shaped)
    return jnp.stack([real_part, imag_part], axis=2).astype(jnp.bfloat16)


def left_plain(coupler, blocks):
    return jnp.einsum("ab,ecbd->ecad", coupler, blocks, preferred_element_type=jnp.float32).astype(
        jnp.bfloat16
    )


def left_transposed(coupler, blocks):
    return jnp.einsum("ba,ecbd->ecad", coupler, blocks, preferred_element_type=jnp.float32).astype(
        jnp.bfloat16
    )


def right_transposed(left, coupler):
    return jnp.einsum("ecad,fd->ecaf", left, coupler, preferred_element_type=jnp.float32)


def right_plain(left, coupler):
    return jnp.einsum("ecad,df->ecaf", left, coupler, preferred_element_type=jnp.float32)


def per_device(lesser, greater, coulomb_diag, coulomb_upper):
    greater_t = jnp.swapaxes(greater, 3, 4)
    lesser_x, greater_x = (
        lax.all_to_all(lesser, "energy", split_axis=3, concat_axis=0, tiled=True),
        lax.all_to_all(greater_t, "energy", split_axis=3, concat_axis=0, tiled=True),
    )
    polar_x = correlate(lesser_x, greater_x)
    polar = lax.all_to_all(polar_x, "energy", split_axis=0, concat_axis=3, tiled=True)
    own = polar[:, 0]
    diag_block = coulomb_diag[0]
    upper_block = coulomb_upper[0]
    total = right_transposed(left_plain(diag_block, own), diag_block)
    polar_next = from_behind(polar, "space", -1)
    outgoing = right_plain(left_transposed(upper_block, own), upper_block)
    total = total + right_transposed(left_plain(upper_block, polar_next[:, 0]), upper_block)
    incoming = from_behind(outgoing.astype(jnp.bfloat16), "space", 1).astype(outgoing.dtype)
    total = total + incoming
    return total.astype(jnp.bfloat16)[:, None]


LAGS = 8
STEPS = 4
LANES = 128
MESH = pl.DeviceIdType.MESH


def to_energy(dest):
    return {"energy": dest}


def correlate_chunk(chunk, energies, lx, hx, lf, hf, cf, cx):
    rows = lf.shape[2]
    flat = (energies, rows, LANES)
    for part_of, held in ((lx, lf), (hx, hf)):
        re = part_of[chunk, :, :, 0].reshape(flat).astype(jnp.float32)
        im = part_of[chunk, :, :, 1].reshape(flat).astype(jnp.float32)
        held[0, pl.ds(0, energies)] = re
        held[1, pl.ds(0, energies)] = im
        held[2, pl.ds(0, energies)] = re + im
    factor = float(energies) ** -0.5

    def one_slab(slab, carry):
        at = pl.ds(pl.multiple_of(slab * 8, 8), 8)
        for first in range(0, energies, LAGS):
            def step(turn, sums):
                start = turn * STEPS
                sums = list(sums)
                for q in range(3):
                    window = [lf[q, start + (first + t), at, :] for t in range(LAGS + STEPS - 1)]
                    taps = [hf[q, start + u, at, :] for u in range(STEPS)]
                    for u in range(STEPS):
                        for j in range(LAGS):
                            sums[q * LAGS + j] = sums[q * LAGS + j] + window[j + u] * taps[u]
                return tuple(sums)

            zero = jnp.zeros((8, LANES), jnp.float32)
            sums = lax.fori_loop(0, (energies - first) // STEPS, step, (zero,) * (3 * LAGS))
            for j in range(LAGS):
                rr, ii, mixed = sums[j], sums[LAGS + j], sums[2 * LAGS + j]
                cf[first + j, 0, at, :] = (mixed - rr - ii) * factor
                cf[first + j, 1, at, :] = (ii - rr) * factor
        return carry

    lax.fori_loop(0, rows // 8, one_slab, 0)
    cx[chunk] = cf[...].astype(jnp.bfloat16).reshape(cx.shape[1:])


def kernel(
    n, ns, lesser, greater, diag_hbm, upper_hbm, out,
    diag, upper, gv, ht, lx, hx, lf, hf, cf, cx, polar, side, uprev, wside, total,
    local_sem, send_sem, recv_l, recv_h, recv_p, side_send, side_recv, u_send, u_recv,
):
    me = lax.axis_index("energy")
    row = lax.axis_index("space")
    chunks, _, k, _, rows, _ = lx.shape
    energies = n * k
    has_next = row < ns - 1
    has_prev = row > 0

    barrier = pltpu.get_barrier_semaphore()

    def greet(step, carry):
        pl.semaphore_signal(
            barrier, inc=1, device_id=to_energy(lax.rem(me + step, n)), device_id_type=MESH
        )
        return carry

    lax.fori_loop(1, n, greet, 0)

    @pl.when(has_next)
    def _():
        pl.semaphore_signal(barrier, inc=1, device_id={"space": row + 1}, device_id_type=MESH)

    @pl.when(has_prev)
    def _():
        pl.semaphore_signal(barrier, inc=1, device_id={"space": row - 1}, device_id_type=MESH)

    load = pltpu.make_async_copy(greater.at[:, 0], gv, local_sem.at[0])
    load.start()
    load_upper = pltpu.make_async_copy(upper_hbm, upper, local_sem.at[1])
    load_upper.start()
    load_diag = pltpu.make_async_copy(diag_hbm, diag, local_sem.at[2])
    load_diag.start()
    load.wait()
    for e in range(k):
        for part_at in range(2):
            ht[e, part_at] = gv[e, part_at].T

    zeros = jnp.zeros((lf.shape[1] - energies,) + lf.shape[2:], jnp.float32)
    for q in range(3):
        lf[q, pl.ds(energies, lf.shape[1] - energies)] = zeros

    pl.semaphore_wait(
        barrier, n - 1 + has_next.astype(jnp.int32) + has_prev.astype(jnp.int32)
    )

    def scatter(source, held, c, kind, recv):
        cols = pl.ds(c * LANES, LANES)

        def part(dest):
            return source.at[:, :, pl.ds(pl.multiple_of(dest * rows, rows), rows), cols]

        def push(step, carry):
            dest = lax.rem(me + step, n)
            pltpu.make_async_remote_copy(
                src_ref=part(dest), dst_ref=held.at[c, me], send_sem=send_sem.at[kind],
                recv_sem=recv.at[c], device_id=to_energy(dest), device_id_type=MESH,
            ).start()
            return carry

        lax.fori_loop(1, n, push, 0)
        pltpu.make_async_copy(part(me), held.at[c, me], recv.at[c]).start()

    u_copy = pltpu.make_async_remote_copy(
        src_ref=upper_hbm.at[0], dst_ref=uprev, send_sem=u_send, recv_sem=u_recv,
        device_id={"space": lax.rem(row + 1, ns)}, device_id_type=MESH,
    )

    @pl.when(has_next)
    def _():
        u_copy.start()

    scatter(lesser.at[:, 0], lx, 0, 0, recv_l)
    scatter(ht, hx, 0, 1, recv_h)
    for c in range(1, chunks):
        scatter(lesser.at[:, 0], lx, c, 0, recv_l)
        scatter(ht, hx, c, 1, recv_h)

    load_upper.wait()
    load_diag.wait()
    wside[0] = upper[0]

    @pl.when(has_prev)
    def _():
        u_copy.wait_recv()
        wside[1] = uprev[...].T

    def one_chunk(c, carry):
        pltpu.make_async_copy(lx.at[c], lx.at[c], recv_l.at[c]).wait()
        pltpu.make_async_copy(hx.at[c], hx.at[c], recv_h.at[c]).wait()
        correlate_chunk(c, energies, lx, hx, lf, hf, cf, cx)
        mine = pl.ds(pl.multiple_of(me * rows, rows), rows)

        def push(step, carry_in):
            dest = lax.rem(me + step, n)
            pltpu.make_async_remote_copy(
                src_ref=cx.at[c, dest], dst_ref=polar.at[c, :, :, mine, :],
                send_sem=send_sem.at[2], recv_sem=recv_p.at[c],
                device_id=to_energy(dest), device_id_type=MESH,
            ).start()
            return carry_in

        lax.fori_loop(1, n, push, 0)
        pltpu.make_async_copy(cx.at[c, me], polar.at[c, :, :, mine, :], recv_p.at[c]).start()
        return carry

    lax.fori_loop(0, chunks, one_chunk, 0)

    def screen(block, coupler, slot, c, begin):
        right = coupler[:, c * LANES:(c + 1) * LANES]
        for e in range(k):
            pair = jnp.concatenate([block[slot, e, 0], block[slot, e, 1]], axis=1)
            left = jnp.dot(coupler, pair, preferred_element_type=jnp.float32).astype(jnp.bfloat16)
            for part_at in range(2):
                term = lax.dot_general(
                    left[:, part_at * LANES:(part_at + 1) * LANES], right,
                    (((1,), (1,)), ((), ())), preferred_element_type=jnp.float32,
                )
                if begin:
                    total[e, part_at] = term
                else:
                    total[e, part_at] += term

    def forward(c, slot, to):
        return pltpu.make_async_remote_copy(
            src_ref=polar.at[c], dst_ref=side.at[slot, c], send_sem=side_send.at[slot, c],
            recv_sem=side_recv.at[slot, c], device_id={"space": to}, device_id_type=MESH,
        )

    up, down = lax.rem(row + 1, ns), lax.rem(row + ns - 1, ns)
    for c in range(chunks):
        pltpu.make_async_copy(polar.at[c], polar.at[c], recv_p.at[c]).wait()

        @pl.when(has_prev)
        def _():
            forward(c, 0, down).start()

        @pl.when(has_next)
        def _():
            forward(c, 1, up).start()

        screen(polar, diag[0], c, c, c == 0)

        @pl.when(has_next)
        def _():
            forward(c, 0, down).wait_recv()
            screen(side.at[0], wside[0], c, c, False)

        @pl.when(has_prev)
        def _():
            forward(c, 1, up).wait_recv()
            screen(side.at[1], wside[1], c, c, False)

    out[:, 0] = total[...].astype(jnp.bfloat16)

    for c in range(chunks):
        @pl.when(has_prev)
        def _():
            forward(c, 0, down).wait_send()

        @pl.when(has_next)
        def _():
            forward(c, 1, up).wait_send()

    @pl.when(has_next)
    def _():
        u_copy.wait_send()

    for kind in range(3):
        sent = lx.at[:, pl.ds(0, n - 1)]
        pltpu.make_async_copy(sent, sent, send_sem.at[kind]).wait()


def fused(n, ns, lesser, greater, diag, upper):
    k, _, _, size, _ = lesser.shape
    rows, chunks, energies = size // n, size // LANES, n * k
    bf, f32 = jnp.bfloat16, jnp.float32
    whole = (k, 2, size, size)
    padded = energies + LAGS + STEPS
    dma = pltpu.SemaphoreType.DMA
    vmem = pl.BlockSpec(memory_space=pltpu.VMEM)
    hbm = pl.BlockSpec(memory_space=pltpu.HBM)
    return pl.pallas_call(
        functools.partial(kernel, n, ns),
        out_shape=jax.ShapeDtypeStruct(lesser.shape, bf),
        in_specs=[hbm] * 4,
        out_specs=vmem,
        scratch_shapes=[
            pltpu.VMEM(diag.shape, bf),
            pltpu.VMEM(upper.shape, bf),
            pltpu.VMEM(whole, bf),
            pltpu.VMEM(whole, bf),
            pltpu.VMEM((chunks, n, k, 2, rows, LANES), bf),
            pltpu.VMEM((chunks, n, k, 2, rows, LANES), bf),
            pltpu.VMEM((3, padded, rows, LANES), f32),
            pltpu.VMEM((3, energies, rows, LANES), f32),
            pltpu.VMEM((energies, 2, rows, LANES), f32),
            pltpu.VMEM((chunks, n, k, 2, rows, LANES), bf),
            pltpu.VMEM((chunks, k, 2, size, LANES), bf),
            pltpu.VMEM((2, chunks, k, 2, size, LANES), bf),
            pltpu.VMEM((size, size), bf),
            pltpu.VMEM((2, size, size), bf),
            pltpu.VMEM(whole, f32),
            dma((3,)), dma((3,)), dma((chunks,)), dma((chunks,)), dma((chunks,)),
            dma((2, chunks)), dma((2, chunks)), dma, dma,
        ],
        compiler_params=pltpu.CompilerParams(
            collective_id=0, has_side_effects=True, vmem_limit_bytes=40 << 20
        ),
    )(*(pltpu.with_memory_space_constraint(x, pltpu.HBM) for x in (lesser, greater, diag, upper)))


def fits(n, ns, size, energies):
    return size % n == 0 and (size // n) % 16 == 0 and size % LANES == 0 and energies % LAGS == 0 and ns > 1


def either(n, ns, lesser, greater, diag, upper):
    if fits(n, ns, lesser.shape[3], n * lesser.shape[0]):
        return fused(n, ns, lesser, greater, diag, upper)
    return per_device(lesser, greater, diag, upper)


def solution(mesh):
    placed = (
        P("energy", "space", None, None, None),
        P("energy", "space", None, None, None),
        P("space", None, None),
        P("space", None, None),
    )
    return jax.shard_map(
        functools.partial(either, mesh.shape["energy"], mesh.shape["space"]),
        mesh=mesh,
        in_specs=placed,
        out_specs=P("energy", "space", None, None, None),
        check_vma=False,
    )
```

```python
import functools
import math

import jax
import jax.numpy as jnp
from jax import lax
from jax.experimental import pallas as pl
from jax.experimental.pallas import tpu as pltpu
from jax.sharding import PartitionSpec as P


def from_behind(value, axis, steps):
    count = lax.axis_size(axis)
    leading, last = (max(0, -steps), min(count, count - steps))
    return lax.ppermute(value, axis, [(source, source + steps) for source in range(leading, last)])


def split_parts(values):
    high = values.astype(jnp.bfloat16)
    low = (values - high.astype(jnp.float32)).astype(jnp.bfloat16)
    return (high, low)


def product_two(table, data_bf):
    return jnp.dot(table[0], data_bf, preferred_element_type=jnp.float32) + jnp.dot(
        table[1], data_bf, preferred_element_type=jnp.float32
    )


def product_three(table, data_f32):
    data_high, data_low = split_parts(data_f32)
    total = jnp.dot(table[0], data_high, preferred_element_type=jnp.float32)
    total = total + jnp.dot(table[1], data_high, preferred_element_type=jnp.float32)
    return total + jnp.dot(table[0], data_low, preferred_element_type=jnp.float32)


def correlate(lesser_x, greater_x):
    energies = lesser_x.shape[0]
    length = 2 * energies
    tail_shape = lesser_x.shape[1:]

    def flatten(values, part):
        return values[:, :, part].reshape(energies, -1)

    lesser_re = flatten(lesser_x, 0)
    lesser_im = flatten(lesser_x, 1)
    greater_re = flatten(greater_x, 0)
    greater_im = flatten(greater_x, 1)
    freqs = lax.broadcasted_iota(jnp.int32, (length, energies), 0)
    places = lax.broadcasted_iota(jnp.int32, (length, energies), 1)
    angles = 2.0 * math.pi / length * jnp.mod(freqs * places, length).astype(jnp.float32)
    cosine = split_parts(jnp.cos(angles))
    sine = split_parts(jnp.sin(angles))
    cosine_t = split_parts(jnp.cos(angles).T)
    sine_t = split_parts(jnp.sin(angles).T)
    hat_lre = product_two(cosine, lesser_re) + product_two(sine, lesser_im)
    hat_lim = product_two(cosine, lesser_im) - product_two(sine, lesser_re)
    hat_gre = product_two(cosine, greater_re) - product_two(sine, greater_im)
    hat_gim = product_two(cosine, greater_im) + product_two(sine, greater_re)
    prod_re = hat_lre * hat_gre - hat_lim * hat_gim
    prod_im = hat_lre * hat_gim + hat_lim * hat_gre
    corr_re = (product_three(cosine_t, prod_re) - product_three(sine_t, prod_im)) / length
    corr_im = (product_three(cosine_t, prod_im) + product_three(sine_t, prod_re)) / length
    factor = jnp.float32(energies) ** (-0.5)
    shaped = (energies, tail_shape[0], tail_shape[2], tail_shape[3])
    real_part = (corr_im * factor).reshape(shaped)
    imag_part = (-corr_re * factor).reshape(shaped)
    return jnp.stack([real_part, imag_part], axis=2).astype(jnp.bfloat16)


def left_plain(coupler, blocks):
    return jnp.einsum("ab,ecbd->ecad", coupler, blocks, preferred_element_type=jnp.float32).astype(
        jnp.bfloat16
    )


def left_transposed(coupler, blocks):
    return jnp.einsum("ba,ecbd->ecad", coupler, blocks, preferred_element_type=jnp.float32).astype(
        jnp.bfloat16
    )


def right_transposed(left, coupler):
    return jnp.einsum("ecad,fd->ecaf", left, coupler, preferred_element_type=jnp.float32)


def right_plain(left, coupler):
    return jnp.einsum("ecad,df->ecaf", left, coupler, preferred_element_type=jnp.float32)


def per_device(lesser, greater, coulomb_diag, coulomb_upper):
    greater_t = jnp.swapaxes(greater, 3, 4)
    lesser_x, greater_x = (
        lax.all_to_all(lesser, "energy", split_axis=3, concat_axis=0, tiled=True),
        lax.all_to_all(greater_t, "energy", split_axis=3, concat_axis=0, tiled=True),
    )
    polar_x = correlate(lesser_x, greater_x)
    polar = lax.all_to_all(polar_x, "energy", split_axis=0, concat_axis=3, tiled=True)
    own = polar[:, 0]
    diag_block = coulomb_diag[0]
    upper_block = coulomb_upper[0]
    total = right_transposed(left_plain(diag_block, own), diag_block)
    polar_next = from_behind(polar, "space", -1)
    outgoing = right_plain(left_transposed(upper_block, own), upper_block)
    total = total + right_transposed(left_plain(upper_block, polar_next[:, 0]), upper_block)
    incoming = from_behind(outgoing.astype(jnp.bfloat16), "space", 1).astype(outgoing.dtype)
    total = total + incoming
    return total.astype(jnp.bfloat16)[:, None]


LAGS = 8
STEPS = 4
LANES = 128
MESH = pl.DeviceIdType.MESH


def to_energy(dest):
    return {"energy": dest}


def widen_into(held, at, re, im):
    re, im = re.astype(jnp.float32), im.astype(jnp.float32)
    held[0, at] = re
    held[1, at] = im
    held[2, at] = re + im


def correlate_into(cf, lf, hf, bounds):
    energies, _, rows, _ = cf.shape
    factor = float(energies) ** -0.5

    def one_slab(slab, carry):
        at = pl.ds(pl.multiple_of(slab * 8, 8), 8)
        for first in range(0, energies, LAGS):
            def step(turn, sums):
                start = turn * STEPS
                sums = list(sums)
                for q in range(3):
                    window = [lf[q, start + (first + t), at, :] for t in range(LAGS + STEPS - 1)]
                    taps = [hf[q, start + u, at, :] for u in range(STEPS)]
                    for u in range(STEPS):
                        for j in range(LAGS):
                            sums[q * LAGS + j] = sums[q * LAGS + j] + window[j + u] * taps[u]
                return tuple(sums)

            zero = jnp.zeros((8, LANES), jnp.float32)
            low, high = bounds(first)
            sums = lax.fori_loop(low, high, step, (zero,) * (3 * LAGS))
            for j in range(LAGS):
                rr, ii, mixed = sums[j], sums[LAGS + j], sums[2 * LAGS + j]
                cf[first + j, 0, at, :] = (mixed - rr - ii) * factor
                cf[first + j, 1, at, :] = (ii - rr) * factor
        return carry

    lax.fori_loop(0, rows // 8, one_slab, 0)


def kernel(
    n, ns, lesser, greater, diag_hbm, upper_hbm, out,
    diag, upper, gv, ht, lx, hx, lf, hf, cf, cx, polar, side, uprev, wside, total,
    lxb, hxb, lfb, hfb, cfb, cxb, partial,
    local_sem, send_sem, recv_l, recv_h, recv_p, side_send, side_recv, u_send, u_recv, half_send, half_recv,
):
    me = lax.axis_index("energy")
    row = lax.axis_index("space")
    chunks, _, k, _, rows, _ = lx.shape
    energies = n * k
    has_next = row < ns - 1
    has_prev = row > 0
    peers = n // 2
    half, member = me // peers, lax.rem(me, peers)
    own_energies = peers * k
    brows = lxb.shape[3]
    upper_half, lower_half = half == 1, half == 0

    barrier = pltpu.get_barrier_semaphore()

    def greet(step, carry):
        pl.semaphore_signal(
            barrier, inc=1, device_id=to_energy(lax.rem(me + step, n)), device_id_type=MESH
        )
        return carry

    lax.fori_loop(1, n, greet, 0)

    @pl.when(has_next)
    def _():
        pl.semaphore_signal(barrier, inc=1, device_id={"space": row + 1}, device_id_type=MESH)

    @pl.when(has_prev)
    def _():
        pl.semaphore_signal(barrier, inc=1, device_id={"space": row - 1}, device_id_type=MESH)

    load = pltpu.make_async_copy(greater.at[:, 0], gv, local_sem.at[0])
    load.start()
    load_upper = pltpu.make_async_copy(upper_hbm, upper, local_sem.at[1])
    load_upper.start()
    load_diag = pltpu.make_async_copy(diag_hbm, diag, local_sem.at[2])
    load_diag.start()
    load.wait()
    for e in range(k):
        for part_at in range(2):
            ht[e, part_at] = gv[e, part_at].T

    zeros = jnp.zeros((lf.shape[1] - energies,) + lf.shape[2:], jnp.float32)
    for q in range(3):
        lf[q, pl.ds(energies, lf.shape[1] - energies)] = zeros
    lfb[...] = jnp.zeros(lfb.shape, jnp.float32)

    pl.semaphore_wait(
        barrier, n - 1 + has_next.astype(jnp.int32) + has_prev.astype(jnp.int32)
    )

    def scatter(source, held, c, kind, recv):
        cols = pl.ds(c * LANES, LANES)

        def part(dest):
            return source.at[:, :, pl.ds(pl.multiple_of(dest * rows, rows), rows), cols]

        def push(step, carry):
            dest = lax.rem(me + step, n)
            pltpu.make_async_remote_copy(
                src_ref=part(dest), dst_ref=held.at[c, me], send_sem=send_sem.at[kind],
                recv_sem=recv.at[c], device_id=to_energy(dest), device_id_type=MESH,
            ).start()
            return carry

        lax.fori_loop(1, n, push, 0)
        pltpu.make_async_copy(part(me), held.at[c, me], recv.at[c]).start()

    u_copy = pltpu.make_async_remote_copy(
        src_ref=upper_hbm.at[0], dst_ref=uprev, send_sem=u_send, recv_sem=u_recv,
        device_id={"space": lax.rem(row + 1, ns)}, device_id_type=MESH,
    )

    @pl.when(has_next)
    def _():
        u_copy.start()

    def spread(pick, land, at_half, begin, kind):
        def push(step, carry):
            peer = lax.rem(member + step, peers)
            dest = at_half * peers + peer
            pltpu.make_async_remote_copy(
                src_ref=pick(dest, peer), dst_ref=land(me, member), send_sem=half_send.at[kind],
                recv_sem=half_recv.at[kind], device_id=to_energy(dest), device_id_type=MESH,
            ).start()
            return carry

        lax.fori_loop(begin, peers, push, 0)
        if begin:
            pltpu.make_async_copy(pick(me, member), land(me, member), half_recv.at[kind]).start()

    def band(source):
        return lambda dest, peer: source.at[
            :, :, pl.ds(pl.multiple_of(peer * brows, brows), brows), pl.ds(0, LANES)
        ]

    @pl.when(lower_half)
    def _():
        spread(band(ht), lambda at, peer: hxb.at[at], 1, 0, 2)

    spread(band(lesser.at[:, 0]), lambda at, peer: lxb.at[at], half, 1, 0)
    spread(band(ht), lambda at, peer: hxb.at[at], half, 1, 1)
    for c in range(1, chunks):
        scatter(lesser.at[:, 0], lx, c, 0, recv_l)
        scatter(ht, hx, c, 1, recv_h)

    load_upper.wait()
    load_diag.wait()
    wside[0] = upper[0]

    @pl.when(has_prev)
    def _():
        u_copy.wait_recv()
        wside[1] = uprev[...].T

    def arrived(buffer, kind):
        pltpu.make_async_copy(buffer, buffer, half_recv.at[kind]).wait()

    some = pl.ds(0, peers)
    own = pl.ds(half * peers, peers)
    own_at = pl.ds(half * own_energies, own_energies)
    short = (own_energies, brows, LANES)
    arrived(lxb.at[some], 0)
    widen_into(lfb, own_at, lxb[own, :, 0].reshape(short), lxb[own, :, 1].reshape(short))
    arrived(hxb.at[some], 1)
    widen_into(hfb, own_at, hxb[own, :, 0].reshape(short), hxb[own, :, 1].reshape(short))

    @pl.when(upper_half)
    def _():
        arrived(hxb.at[some], 2)
        widen_into(
            hfb, pl.ds(0, own_energies), hxb[some, :, 0].reshape(short), hxb[some, :, 1].reshape(short)
        )

    def half_bounds(first):
        begin = max(0, (own_energies - first - (LAGS + STEPS - 2)) // STEPS)
        low_end, high_end = max(0, own_energies - first) // STEPS, (energies - first) // STEPS
        return half * begin, low_end + half * (high_end - low_end)

    correlate_into(cfb, lfb, hfb, half_bounds)
    cxb[...] = cfb[...].astype(jnp.bfloat16).reshape(cxb.shape)

    def landing(buffer):
        return lambda at, peer: buffer.at[:, :, pl.ds(pl.multiple_of(peer * brows, brows), brows), :]

    @pl.when(upper_half)
    def _():
        spread(lambda dest, peer: cxb.at[dest], landing(partial), 0, 0, 4)

    spread(lambda dest, peer: cxb.at[dest], landing(polar.at[0]), half, 1, 3)

    def one_chunk(c, carry):
        pltpu.make_async_copy(lx.at[c], lx.at[c], recv_l.at[c]).wait()
        pltpu.make_async_copy(hx.at[c], hx.at[c], recv_h.at[c]).wait()
        flat = (energies, rows, LANES)
        for held, wide in ((lx, lf), (hx, hf)):
            widen_into(wide, pl.ds(0, energies), held[c, :, :, 0].reshape(flat), held[c, :, :, 1].reshape(flat))
        correlate_into(cf, lf, hf, lambda first: (0, (energies - first) // STEPS))
        cx[c] = cf[...].astype(jnp.bfloat16).reshape(cx.shape[1:])
        mine = pl.ds(pl.multiple_of(me * rows, rows), rows)

        def push(step, carry_in):
            dest = lax.rem(me + step, n)
            pltpu.make_async_remote_copy(
                src_ref=cx.at[c, dest], dst_ref=polar.at[c, :, :, mine, :],
                send_sem=send_sem.at[2], recv_sem=recv_p.at[c],
                device_id=to_energy(dest), device_id_type=MESH,
            ).start()
            return carry_in

        lax.fori_loop(1, n, push, 0)
        pltpu.make_async_copy(cx.at[c, me], polar.at[c, :, :, mine, :], recv_p.at[c]).start()
        return carry

    lax.fori_loop(1, chunks, one_chunk, 0)

    def screen(block, coupler, slot, c, begin):
        right = coupler[:, c * LANES:(c + 1) * LANES]
        for e in range(k):
            pair = jnp.concatenate([block[slot, e, 0], block[slot, e, 1]], axis=1)
            left = jnp.dot(coupler, pair, preferred_element_type=jnp.float32).astype(jnp.bfloat16)
            for part_at in range(2):
                term = lax.dot_general(
                    left[:, part_at * LANES:(part_at + 1) * LANES], right,
                    (((1,), (1,)), ((), ())), preferred_element_type=jnp.float32,
                )
                if begin:
                    total[e, part_at] = term
                else:
                    total[e, part_at] += term

    def forward(c, slot, to):
        return pltpu.make_async_remote_copy(
            src_ref=polar.at[c], dst_ref=side.at[slot, c], send_sem=side_send.at[slot, c],
            recv_sem=side_recv.at[slot, c], device_id={"space": to}, device_id_type=MESH,
        )

    up, down = lax.rem(row + 1, ns), lax.rem(row + ns - 1, ns)
    for c in range(chunks):
        if c:
            pltpu.make_async_copy(polar.at[c], polar.at[c], recv_p.at[c]).wait()
        else:
            arrived(polar.at[0], 3)

            @pl.when(lower_half)
            def _():
                arrived(partial, 4)
                both = polar[0].astype(jnp.float32) + partial[...].astype(jnp.float32)
                polar[0] = both.astype(jnp.bfloat16)

        @pl.when(has_prev)
        def _():
            forward(c, 0, down).start()

        @pl.when(has_next)
        def _():
            forward(c, 1, up).start()

        screen(polar, diag[0], c, c, c == 0)

        @pl.when(has_next)
        def _():
            forward(c, 0, down).wait_recv()
            screen(side.at[0], wside[0], c, c, False)

        @pl.when(has_prev)
        def _():
            forward(c, 1, up).wait_recv()
            screen(side.at[1], wside[1], c, c, False)

    out[:, 0] = total[...].astype(jnp.bfloat16)

    for c in range(chunks):
        @pl.when(has_prev)
        def _():
            forward(c, 0, down).wait_send()

        @pl.when(has_next)
        def _():
            forward(c, 1, up).wait_send()

    @pl.when(has_next)
    def _():
        u_copy.wait_send()

    for kind in range(3):
        sent = lx.at[pl.ds(1, chunks - 1), pl.ds(0, n - 1)]
        pltpu.make_async_copy(sent, sent, send_sem.at[kind]).wait()

    def left_here(count, kind):
        sent = lxb.at[pl.ds(0, count)]
        pltpu.make_async_copy(sent, sent, half_send.at[kind]).wait()

    for kind in (0, 1, 3):
        left_here(peers - 1, kind)

    @pl.when(lower_half)
    def _():
        left_here(peers, 2)

    @pl.when(upper_half)
    def _():
        left_here(peers, 4)


def fused(n, ns, lesser, greater, diag, upper):
    k, _, _, size, _ = lesser.shape
    rows, chunks, energies = size // n, size // LANES, n * k
    bf, f32 = jnp.bfloat16, jnp.float32
    whole = (k, 2, size, size)
    padded = energies + LAGS + STEPS
    dma = pltpu.SemaphoreType.DMA
    vmem = pl.BlockSpec(memory_space=pltpu.VMEM)
    hbm = pl.BlockSpec(memory_space=pltpu.HBM)
    return pl.pallas_call(
        functools.partial(kernel, n, ns),
        out_shape=jax.ShapeDtypeStruct(lesser.shape, bf),
        in_specs=[hbm] * 4,
        out_specs=vmem,
        scratch_shapes=[
            pltpu.VMEM(diag.shape, bf),
            pltpu.VMEM(upper.shape, bf),
            pltpu.VMEM(whole, bf),
            pltpu.VMEM(whole, bf),
            pltpu.VMEM((chunks, n, k, 2, rows, LANES), bf),
            pltpu.VMEM((chunks, n, k, 2, rows, LANES), bf),
            pltpu.VMEM((3, padded, rows, LANES), f32),
            pltpu.VMEM((3, energies, rows, LANES), f32),
            pltpu.VMEM((energies, 2, rows, LANES), f32),
            pltpu.VMEM((chunks, n, k, 2, rows, LANES), bf),
            pltpu.VMEM((chunks, k, 2, size, LANES), bf),
            pltpu.VMEM((2, chunks, k, 2, size, LANES), bf),
            pltpu.VMEM((size, size), bf),
            pltpu.VMEM((2, size, size), bf),
            pltpu.VMEM(whole, f32),
            pltpu.VMEM((n, k, 2, 2 * rows, LANES), bf),
            pltpu.VMEM((n, k, 2, 2 * rows, LANES), bf),
            pltpu.VMEM((3, padded, 2 * rows, LANES), f32),
            pltpu.VMEM((3, energies, 2 * rows, LANES), f32),
            pltpu.VMEM((energies, 2, 2 * rows, LANES), f32),
            pltpu.VMEM((n, k, 2, 2 * rows, LANES), bf),
            pltpu.VMEM((k, 2, size, LANES), bf),
            dma((3,)), dma((3,)), dma((chunks,)), dma((chunks,)), dma((chunks,)),
            dma((2, chunks)), dma((2, chunks)), dma, dma,
            dma((5,)), dma((5,)),
        ],
        compiler_params=pltpu.CompilerParams(
            collective_id=0, has_side_effects=True, vmem_limit_bytes=40 << 20
        ),
    )(*(pltpu.with_memory_space_constraint(x, pltpu.HBM) for x in (lesser, greater, diag, upper)))


def fits(n, ns, size, energies):
    banded = n % 2 == 0 and size % n == 0 and (size // n) % 16 == 0 and size % LANES == 0
    return banded and size > LANES and energies % (2 * LAGS) == 0 and ns > 1


def either(n, ns, lesser, greater, diag, upper):
    if fits(n, ns, lesser.shape[3], n * lesser.shape[0]):
        return fused(n, ns, lesser, greater, diag, upper)
    return per_device(lesser, greater, diag, upper)


def solution(mesh):
    placed = (
        P("energy", "space", None, None, None),
        P("energy", "space", None, None, None),
        P("space", None, None),
        P("space", None, None),
    )
    return jax.shard_map(
        functools.partial(either, mesh.shape["energy"], mesh.shape["space"]),
        mesh=mesh,
        in_specs=placed,
        out_specs=P("energy", "space", None, None, None),
        check_vma=False,
    )
```

```python
import functools
import math

import jax
import jax.numpy as jnp
from jax import lax
from jax.experimental import pallas as pl
from jax.experimental.pallas import tpu as pltpu
from jax.sharding import PartitionSpec as P


def from_behind(value, axis, steps):
    count = lax.axis_size(axis)
    leading, last = (max(0, -steps), min(count, count - steps))
    return lax.ppermute(value, axis, [(source, source + steps) for source in range(leading, last)])


def split_parts(values):
    high = values.astype(jnp.bfloat16)
    low = (values - high.astype(jnp.float32)).astype(jnp.bfloat16)
    return (high, low)


def product_two(table, data_bf):
    return jnp.dot(table[0], data_bf, preferred_element_type=jnp.float32) + jnp.dot(
        table[1], data_bf, preferred_element_type=jnp.float32
    )


def product_three(table, data_f32):
    data_high, data_low = split_parts(data_f32)
    total = jnp.dot(table[0], data_high, preferred_element_type=jnp.float32)
    total = total + jnp.dot(table[1], data_high, preferred_element_type=jnp.float32)
    return total + jnp.dot(table[0], data_low, preferred_element_type=jnp.float32)


def correlate(lesser_x, greater_x):
    energies = lesser_x.shape[0]
    length = 2 * energies
    tail_shape = lesser_x.shape[1:]

    def flatten(values, part):
        return values[:, :, part].reshape(energies, -1)

    lesser_re = flatten(lesser_x, 0)
    lesser_im = flatten(lesser_x, 1)
    greater_re = flatten(greater_x, 0)
    greater_im = flatten(greater_x, 1)
    freqs = lax.broadcasted_iota(jnp.int32, (length, energies), 0)
    places = lax.broadcasted_iota(jnp.int32, (length, energies), 1)
    angles = 2.0 * math.pi / length * jnp.mod(freqs * places, length).astype(jnp.float32)
    cosine = split_parts(jnp.cos(angles))
    sine = split_parts(jnp.sin(angles))
    cosine_t = split_parts(jnp.cos(angles).T)
    sine_t = split_parts(jnp.sin(angles).T)
    hat_lre = product_two(cosine, lesser_re) + product_two(sine, lesser_im)
    hat_lim = product_two(cosine, lesser_im) - product_two(sine, lesser_re)
    hat_gre = product_two(cosine, greater_re) - product_two(sine, greater_im)
    hat_gim = product_two(cosine, greater_im) + product_two(sine, greater_re)
    prod_re = hat_lre * hat_gre - hat_lim * hat_gim
    prod_im = hat_lre * hat_gim + hat_lim * hat_gre
    corr_re = (product_three(cosine_t, prod_re) - product_three(sine_t, prod_im)) / length
    corr_im = (product_three(cosine_t, prod_im) + product_three(sine_t, prod_re)) / length
    factor = jnp.float32(energies) ** (-0.5)
    shaped = (energies, tail_shape[0], tail_shape[2], tail_shape[3])
    real_part = (corr_im * factor).reshape(shaped)
    imag_part = (-corr_re * factor).reshape(shaped)
    return jnp.stack([real_part, imag_part], axis=2).astype(jnp.bfloat16)


def left_plain(coupler, blocks):
    return jnp.einsum("ab,ecbd->ecad", coupler, blocks, preferred_element_type=jnp.float32).astype(
        jnp.bfloat16
    )


def left_transposed(coupler, blocks):
    return jnp.einsum("ba,ecbd->ecad", coupler, blocks, preferred_element_type=jnp.float32).astype(
        jnp.bfloat16
    )


def right_transposed(left, coupler):
    return jnp.einsum("ecad,fd->ecaf", left, coupler, preferred_element_type=jnp.float32)


def right_plain(left, coupler):
    return jnp.einsum("ecad,df->ecaf", left, coupler, preferred_element_type=jnp.float32)


def per_device(lesser, greater, coulomb_diag, coulomb_upper):
    greater_t = jnp.swapaxes(greater, 3, 4)
    lesser_x, greater_x = (
        lax.all_to_all(lesser, "energy", split_axis=3, concat_axis=0, tiled=True),
        lax.all_to_all(greater_t, "energy", split_axis=3, concat_axis=0, tiled=True),
    )
    polar_x = correlate(lesser_x, greater_x)
    polar = lax.all_to_all(polar_x, "energy", split_axis=0, concat_axis=3, tiled=True)
    own = polar[:, 0]
    diag_block = coulomb_diag[0]
    upper_block = coulomb_upper[0]
    total = right_transposed(left_plain(diag_block, own), diag_block)
    polar_next = from_behind(polar, "space", -1)
    outgoing = right_plain(left_transposed(upper_block, own), upper_block)
    total = total + right_transposed(left_plain(upper_block, polar_next[:, 0]), upper_block)
    incoming = from_behind(outgoing.astype(jnp.bfloat16), "space", 1).astype(outgoing.dtype)
    total = total + incoming
    return total.astype(jnp.bfloat16)[:, None]


LAGS = 8
STEPS = 4
LANES = 128
MESH = pl.DeviceIdType.MESH


def to_energy(dest):
    return {"energy": dest}


def widen_into(held, at, re, im):
    re, im = re.astype(jnp.float32), im.astype(jnp.float32)
    held[0, at] = re
    held[1, at] = im
    held[2, at] = re + im


def correlate_into(cf, lf, hf, bounds):
    energies, _, rows, _ = cf.shape
    factor = float(energies) ** -0.5

    def one_slab(slab, carry):
        at = pl.ds(pl.multiple_of(slab * 8, 8), 8)
        for first in range(0, energies, LAGS):
            def step(turn, sums):
                start = turn * STEPS
                sums = list(sums)
                for q in range(3):
                    window = [lf[q, start + (first + t), at, :] for t in range(LAGS + STEPS - 1)]
                    taps = [hf[q, start + u, at, :] for u in range(STEPS)]
                    for u in range(STEPS):
                        for j in range(LAGS):
                            sums[q * LAGS + j] = sums[q * LAGS + j] + window[j + u] * taps[u]
                return tuple(sums)

            zero = jnp.zeros((8, LANES), jnp.float32)
            low, high = bounds(first)
            sums = lax.fori_loop(low, high, step, (zero,) * (3 * LAGS))
            for j in range(LAGS):
                rr, ii, mixed = sums[j], sums[LAGS + j], sums[2 * LAGS + j]
                cf[first + j, 0, at, :] = (mixed - rr - ii) * factor
                cf[first + j, 1, at, :] = (ii - rr) * factor
        return carry

    lax.fori_loop(0, rows // 8, one_slab, 0)


def kernel(
    n, ns, lesser, greater, diag_hbm, upper_hbm, out,
    diag, upper, gv, ht, lx, hx, lf, hf, cf, cx, polar, side, uprev, wside, total,
    lxb, hxb, lfb, hfb, cxb, partial,
    local_sem, send_sem, recv_l, recv_h, recv_p, side_send, side_recv, u_send, u_recv, half_send, half_recv,
):
    me = lax.axis_index("energy")
    row = lax.axis_index("space")
    chunks, _, k, _, rows, _ = lx.shape
    energies = n * k
    has_next = row < ns - 1
    has_prev = row > 0
    peers = n // 2
    half, member = me // peers, lax.rem(me, peers)
    own_energies = peers * k
    bands = lxb.shape[0]
    brows = bands * rows
    upper_half, lower_half = half == 1, half == 0

    barrier = pltpu.get_barrier_semaphore()

    def greet(step, carry):
        pl.semaphore_signal(
            barrier, inc=1, device_id=to_energy(lax.rem(me + step, n)), device_id_type=MESH
        )
        return carry

    lax.fori_loop(1, n, greet, 0)

    @pl.when(has_next)
    def _():
        pl.semaphore_signal(barrier, inc=1, device_id={"space": row + 1}, device_id_type=MESH)

    @pl.when(has_prev)
    def _():
        pl.semaphore_signal(barrier, inc=1, device_id={"space": row - 1}, device_id_type=MESH)

    load = pltpu.make_async_copy(greater.at[:, 0], gv, local_sem.at[0])
    load.start()
    load_upper = pltpu.make_async_copy(upper_hbm, upper, local_sem.at[1])
    load_upper.start()
    load_diag = pltpu.make_async_copy(diag_hbm, diag, local_sem.at[2])
    load_diag.start()
    load.wait()
    for e in range(k):
        for part_at in range(2):
            ht[e, part_at] = gv[e, part_at].T

    zeros = jnp.zeros((lf.shape[1] - energies,) + lf.shape[2:], jnp.float32)
    for q in range(3):
        lf[q, pl.ds(energies, lf.shape[1] - energies)] = zeros
    lfb[...] = jnp.zeros(lfb.shape, jnp.float32)

    pl.semaphore_wait(
        barrier, n - 1 + has_next.astype(jnp.int32) + has_prev.astype(jnp.int32)
    )

    def scatter(source, held, c, kind, recv):
        cols = pl.ds(c * LANES, LANES)

        def part(dest):
            return source.at[:, :, pl.ds(pl.multiple_of(dest * rows, rows), rows), cols]

        def push(step, carry):
            dest = lax.rem(me + step, n)
            pltpu.make_async_remote_copy(
                src_ref=part(dest), dst_ref=held.at[c, me], send_sem=send_sem.at[kind],
                recv_sem=recv.at[c], device_id=to_energy(dest), device_id_type=MESH,
            ).start()
            return carry

        lax.fori_loop(1, n, push, 0)
        pltpu.make_async_copy(part(me), held.at[c, me], recv.at[c]).start()

    u_copy = pltpu.make_async_remote_copy(
        src_ref=upper_hbm.at[0], dst_ref=uprev, send_sem=u_send, recv_sem=u_recv,
        device_id={"space": lax.rem(row + 1, ns)}, device_id_type=MESH,
    )

    @pl.when(has_next)
    def _():
        u_copy.start()

    def spread(pick, land, at_half, begin, kind, turn):
        def push(step, carry):
            peer = lax.rem(member + step, peers)
            dest = at_half * peers + peer
            pltpu.make_async_remote_copy(
                src_ref=pick(dest, peer), dst_ref=land(me, member), send_sem=half_send.at[kind],
                recv_sem=half_recv.at[kind, turn], device_id=to_energy(dest), device_id_type=MESH,
            ).start()
            return carry

        lax.fori_loop(begin, peers, push, 0)
        if begin:
            pltpu.make_async_copy(pick(me, member), land(me, member), half_recv.at[kind, turn]).start()

    def band_rows(peer, j):
        return pl.ds(pl.multiple_of(peer * brows + j * rows, rows), rows)

    def band(source, j):
        return lambda dest, peer: source.at[:, :, band_rows(peer, j), pl.ds(0, LANES)]

    def slot(buffer, j):
        return lambda at, peer: buffer.at[j, at]

    @pl.when(lower_half)
    def _():
        for j in range(bands):
            spread(band(ht, j), slot(hxb, j), 1, 0, 2, j)

    for j in range(bands):
        spread(band(lesser.at[:, 0], j), slot(lxb, j), half, 1, 0, j)
        spread(band(ht, j), slot(hxb, j), half, 1, 1, j)
    for c in range(1, chunks):
        scatter(lesser.at[:, 0], lx, c, 0, recv_l)
        scatter(ht, hx, c, 1, recv_h)

    load_upper.wait()
    load_diag.wait()
    wside[0] = upper[0]

    @pl.when(has_prev)
    def _():
        u_copy.wait_recv()
        wside[1] = uprev[...].T

    def arrived(buffer, kind, turn):
        pltpu.make_async_copy(buffer, buffer, half_recv.at[kind, turn]).wait()

    some = pl.ds(0, peers)
    own = pl.ds(half * peers, peers)
    short = (own_energies, rows, LANES)

    def half_bounds(first):
        begin = max(0, (own_energies - first - (LAGS + STEPS - 2)) // STEPS)
        low_end, high_end = max(0, own_energies - first) // STEPS, (energies - first) // STEPS
        return half * begin, low_end + half * (high_end - low_end)

    def landing(buffer, j):
        return lambda at, peer: buffer.at[:, :, band_rows(peer, j), :]

    for j in range(bands):
        own_at = pl.ds(half * own_energies, own_energies)
        arrived(lxb.at[j, some], 0, j)
        widen_into(lfb, own_at, lxb[j, own, :, 0].reshape(short), lxb[j, own, :, 1].reshape(short))
        arrived(hxb.at[j, some], 1, j)
        widen_into(hfb, own_at, hxb[j, own, :, 0].reshape(short), hxb[j, own, :, 1].reshape(short))

        @pl.when(upper_half)
        def _():
            arrived(hxb.at[j, some], 2, j)
            re, im = hxb[j, some, :, 0].reshape(short), hxb[j, some, :, 1].reshape(short)
            widen_into(hfb, pl.ds(0, own_energies), re, im)

        correlate_into(cf, lfb, hfb, half_bounds)
        cxb[j] = cf[...].astype(jnp.bfloat16).reshape(cxb.shape[1:])

        @pl.when(upper_half)
        def _():
            spread(lambda dest, peer: cxb.at[j, dest], landing(partial, j), 0, 0, 4, 0)

        spread(lambda dest, peer: cxb.at[j, dest], landing(polar.at[0], j), half, 1, 3, 0)

    def one_chunk(c, carry):
        pltpu.make_async_copy(lx.at[c], lx.at[c], recv_l.at[c]).wait()
        pltpu.make_async_copy(hx.at[c], hx.at[c], recv_h.at[c]).wait()
        flat = (energies, rows, LANES)
        for held, wide in ((lx, lf), (hx, hf)):
            widen_into(wide, pl.ds(0, energies), held[c, :, :, 0].reshape(flat), held[c, :, :, 1].reshape(flat))
        correlate_into(cf, lf, hf, lambda first: (0, (energies - first) // STEPS))
        cx[c] = cf[...].astype(jnp.bfloat16).reshape(cx.shape[1:])
        mine = pl.ds(pl.multiple_of(me * rows, rows), rows)

        def push(step, carry_in):
            dest = lax.rem(me + step, n)
            pltpu.make_async_remote_copy(
                src_ref=cx.at[c, dest], dst_ref=polar.at[c, :, :, mine, :],
                send_sem=send_sem.at[2], recv_sem=recv_p.at[c],
                device_id=to_energy(dest), device_id_type=MESH,
            ).start()
            return carry_in

        lax.fori_loop(1, n, push, 0)
        pltpu.make_async_copy(cx.at[c, me], polar.at[c, :, :, mine, :], recv_p.at[c]).start()
        return carry

    lax.fori_loop(1, chunks, one_chunk, 0)

    def screen(block, coupler, slot, c, begin):
        right = coupler[:, c * LANES:(c + 1) * LANES]
        for e in range(k):
            pair = jnp.concatenate([block[slot, e, 0], block[slot, e, 1]], axis=1)
            left = jnp.dot(coupler, pair, preferred_element_type=jnp.float32).astype(jnp.bfloat16)
            for part_at in range(2):
                term = lax.dot_general(
                    left[:, part_at * LANES:(part_at + 1) * LANES], right,
                    (((1,), (1,)), ((), ())), preferred_element_type=jnp.float32,
                )
                if begin:
                    total[e, part_at] = term
                else:
                    total[e, part_at] += term

    def forward(c, slot, to):
        return pltpu.make_async_remote_copy(
            src_ref=polar.at[c], dst_ref=side.at[slot, c], send_sem=side_send.at[slot, c],
            recv_sem=side_recv.at[slot, c], device_id={"space": to}, device_id_type=MESH,
        )

    up, down = lax.rem(row + 1, ns), lax.rem(row + ns - 1, ns)
    for c in range(chunks):
        if c:
            pltpu.make_async_copy(polar.at[c], polar.at[c], recv_p.at[c]).wait()
        else:
            arrived(polar.at[0], 3, 0)

            @pl.when(lower_half)
            def _():
                arrived(partial, 4, 0)
                both = polar[0].astype(jnp.float32) + partial[...].astype(jnp.float32)
                polar[0] = both.astype(jnp.bfloat16)

        @pl.when(has_prev)
        def _():
            forward(c, 0, down).start()

        @pl.when(has_next)
        def _():
            forward(c, 1, up).start()

        screen(polar, diag[0], c, c, c == 0)

        @pl.when(has_next)
        def _():
            forward(c, 0, down).wait_recv()
            screen(side.at[0], wside[0], c, c, False)

        @pl.when(has_prev)
        def _():
            forward(c, 1, up).wait_recv()
            screen(side.at[1], wside[1], c, c, False)

    out[:, 0] = total[...].astype(jnp.bfloat16)

    for c in range(chunks):
        @pl.when(has_prev)
        def _():
            forward(c, 0, down).wait_send()

        @pl.when(has_next)
        def _():
            forward(c, 1, up).wait_send()

    @pl.when(has_next)
    def _():
        u_copy.wait_send()

    for kind in range(3):
        sent = lx.at[pl.ds(1, chunks - 1), pl.ds(0, n - 1)]
        pltpu.make_async_copy(sent, sent, send_sem.at[kind]).wait()

    def left_here(count, kind):
        sent = lxb.at[:, pl.ds(0, count)]
        pltpu.make_async_copy(sent, sent, half_send.at[kind]).wait()

    for kind in (0, 1, 3):
        left_here(peers - 1, kind)

    @pl.when(lower_half)
    def _():
        left_here(peers, 2)

    @pl.when(upper_half)
    def _():
        left_here(peers, 4)


def fused(n, ns, lesser, greater, diag, upper):
    k, _, _, size, _ = lesser.shape
    rows, chunks, energies = size // n, size // LANES, n * k
    bf, f32 = jnp.bfloat16, jnp.float32
    whole = (k, 2, size, size)
    padded = energies + LAGS + STEPS
    dma = pltpu.SemaphoreType.DMA
    vmem = pl.BlockSpec(memory_space=pltpu.VMEM)
    hbm = pl.BlockSpec(memory_space=pltpu.HBM)
    return pl.pallas_call(
        functools.partial(kernel, n, ns),
        out_shape=jax.ShapeDtypeStruct(lesser.shape, bf),
        in_specs=[hbm] * 4,
        out_specs=vmem,
        scratch_shapes=[
            pltpu.VMEM(diag.shape, bf),
            pltpu.VMEM(upper.shape, bf),
            pltpu.VMEM(whole, bf),
            pltpu.VMEM(whole, bf),
            pltpu.VMEM((chunks, n, k, 2, rows, LANES), bf),
            pltpu.VMEM((chunks, n, k, 2, rows, LANES), bf),
            pltpu.VMEM((3, padded, rows, LANES), f32),
            pltpu.VMEM((3, energies, rows, LANES), f32),
            pltpu.VMEM((energies, 2, rows, LANES), f32),
            pltpu.VMEM((chunks, n, k, 2, rows, LANES), bf),
            pltpu.VMEM((chunks, k, 2, size, LANES), bf),
            pltpu.VMEM((2, chunks, k, 2, size, LANES), bf),
            pltpu.VMEM((size, size), bf),
            pltpu.VMEM((2, size, size), bf),
            pltpu.VMEM(whole, f32),
            pltpu.VMEM((2, n, k, 2, rows, LANES), bf),
            pltpu.VMEM((2, n, k, 2, rows, LANES), bf),
            pltpu.VMEM((3, padded, rows, LANES), f32),
            pltpu.VMEM((3, energies, rows, LANES), f32),
            pltpu.VMEM((2, n, k, 2, rows, LANES), bf),
            pltpu.VMEM((k, 2, size, LANES), bf),
            dma((3,)), dma((3,)), dma((chunks,)), dma((chunks,)), dma((chunks,)),
            dma((2, chunks)), dma((2, chunks)), dma, dma,
            dma((5,)), dma((5, 2)),
        ],
        compiler_params=pltpu.CompilerParams(
            collective_id=0, has_side_effects=True, vmem_limit_bytes=40 << 20
        ),
    )(*(pltpu.with_memory_space_constraint(x, pltpu.HBM) for x in (lesser, greater, diag, upper)))


def fits(n, ns, size, energies):
    banded = n % 2 == 0 and size % n == 0 and (size // n) % 16 == 0 and size % LANES == 0
    return banded and size > LANES and energies % (2 * LAGS) == 0 and ns > 1


def either(n, ns, lesser, greater, diag, upper):
    if fits(n, ns, lesser.shape[3], n * lesser.shape[0]):
        return fused(n, ns, lesser, greater, diag, upper)
    return per_device(lesser, greater, diag, upper)


def solution(mesh):
    placed = (
        P("energy", "space", None, None, None),
        P("energy", "space", None, None, None),
        P("space", None, None),
        P("space", None, None),
    )
    return jax.shard_map(
        functools.partial(either, mesh.shape["energy"], mesh.shape["space"]),
        mesh=mesh,
        in_specs=placed,
        out_specs=P("energy", "space", None, None, None),
        check_vma=False,
    )
```

```python
import functools
import math

import jax
import jax.numpy as jnp
from jax import lax
from jax.experimental import pallas as pl
from jax.experimental.pallas import tpu as pltpu
from jax.sharding import PartitionSpec as P


def from_behind(value, axis, steps):
    count = lax.axis_size(axis)
    leading, last = (max(0, -steps), min(count, count - steps))
    return lax.ppermute(value, axis, [(source, source + steps) for source in range(leading, last)])


def split_parts(values):
    high = values.astype(jnp.bfloat16)
    low = (values - high.astype(jnp.float32)).astype(jnp.bfloat16)
    return (high, low)


def product_two(table, data_bf):
    return jnp.dot(table[0], data_bf, preferred_element_type=jnp.float32) + jnp.dot(
        table[1], data_bf, preferred_element_type=jnp.float32
    )


def product_three(table, data_f32):
    data_high, data_low = split_parts(data_f32)
    total = jnp.dot(table[0], data_high, preferred_element_type=jnp.float32)
    total = total + jnp.dot(table[1], data_high, preferred_element_type=jnp.float32)
    return total + jnp.dot(table[0], data_low, preferred_element_type=jnp.float32)


def correlate(lesser_x, greater_x):
    energies = lesser_x.shape[0]
    length = 2 * energies
    tail_shape = lesser_x.shape[1:]

    def flatten(values, part):
        return values[:, :, part].reshape(energies, -1)

    lesser_re = flatten(lesser_x, 0)
    lesser_im = flatten(lesser_x, 1)
    greater_re = flatten(greater_x, 0)
    greater_im = flatten(greater_x, 1)
    freqs = lax.broadcasted_iota(jnp.int32, (length, energies), 0)
    places = lax.broadcasted_iota(jnp.int32, (length, energies), 1)
    angles = 2.0 * math.pi / length * jnp.mod(freqs * places, length).astype(jnp.float32)
    cosine = split_parts(jnp.cos(angles))
    sine = split_parts(jnp.sin(angles))
    cosine_t = split_parts(jnp.cos(angles).T)
    sine_t = split_parts(jnp.sin(angles).T)
    hat_lre = product_two(cosine, lesser_re) + product_two(sine, lesser_im)
    hat_lim = product_two(cosine, lesser_im) - product_two(sine, lesser_re)
    hat_gre = product_two(cosine, greater_re) - product_two(sine, greater_im)
    hat_gim = product_two(cosine, greater_im) + product_two(sine, greater_re)
    prod_re = hat_lre * hat_gre - hat_lim * hat_gim
    prod_im = hat_lre * hat_gim + hat_lim * hat_gre
    corr_re = (product_three(cosine_t, prod_re) - product_three(sine_t, prod_im)) / length
    corr_im = (product_three(cosine_t, prod_im) + product_three(sine_t, prod_re)) / length
    factor = jnp.float32(energies) ** (-0.5)
    shaped = (energies, tail_shape[0], tail_shape[2], tail_shape[3])
    real_part = (corr_im * factor).reshape(shaped)
    imag_part = (-corr_re * factor).reshape(shaped)
    return jnp.stack([real_part, imag_part], axis=2).astype(jnp.bfloat16)


def left_plain(coupler, blocks):
    return jnp.einsum("ab,ecbd->ecad", coupler, blocks, preferred_element_type=jnp.float32).astype(
        jnp.bfloat16
    )


def left_transposed(coupler, blocks):
    return jnp.einsum("ba,ecbd->ecad", coupler, blocks, preferred_element_type=jnp.float32).astype(
        jnp.bfloat16
    )


def right_transposed(left, coupler):
    return jnp.einsum("ecad,fd->ecaf", left, coupler, preferred_element_type=jnp.float32)


def right_plain(left, coupler):
    return jnp.einsum("ecad,df->ecaf", left, coupler, preferred_element_type=jnp.float32)


def per_device(lesser, greater, coulomb_diag, coulomb_upper):
    greater_t = jnp.swapaxes(greater, 3, 4)
    lesser_x, greater_x = (
        lax.all_to_all(lesser, "energy", split_axis=3, concat_axis=0, tiled=True),
        lax.all_to_all(greater_t, "energy", split_axis=3, concat_axis=0, tiled=True),
    )
    polar_x = correlate(lesser_x, greater_x)
    polar = lax.all_to_all(polar_x, "energy", split_axis=0, concat_axis=3, tiled=True)
    own = polar[:, 0]
    diag_block = coulomb_diag[0]
    upper_block = coulomb_upper[0]
    total = right_transposed(left_plain(diag_block, own), diag_block)
    polar_next = from_behind(polar, "space", -1)
    outgoing = right_plain(left_transposed(upper_block, own), upper_block)
    total = total + right_transposed(left_plain(upper_block, polar_next[:, 0]), upper_block)
    incoming = from_behind(outgoing.astype(jnp.bfloat16), "space", 1).astype(outgoing.dtype)
    total = total + incoming
    return total.astype(jnp.bfloat16)[:, None]


LAGS = 8
STEPS = 4
LANES = 128
MESH = pl.DeviceIdType.MESH


def to_energy(dest):
    return {"energy": dest}


def widen_into(held, at, re, im):
    re, im = re.astype(jnp.float32), im.astype(jnp.float32)
    held[0, at] = re
    held[1, at] = im
    held[2, at] = re + im


def correlate_into(cf, lf, hf, bounds):
    energies, _, rows, _ = cf.shape
    factor = float(energies) ** -0.5

    def one_slab(slab, carry):
        at = pl.ds(pl.multiple_of(slab * 8, 8), 8)
        for first in range(0, energies, LAGS):
            def step(turn, sums):
                start = turn * STEPS
                sums = list(sums)
                for q in range(3):
                    window = [lf[q, start + (first + t), at, :] for t in range(LAGS + STEPS - 1)]
                    taps = [hf[q, start + u, at, :] for u in range(STEPS)]
                    for u in range(STEPS):
                        for j in range(LAGS):
                            sums[q * LAGS + j] = sums[q * LAGS + j] + window[j + u] * taps[u]
                return tuple(sums)

            zero = jnp.zeros((8, LANES), jnp.float32)
            low, high = bounds(first)
            sums = lax.fori_loop(low, high, step, (zero,) * (3 * LAGS))
            for j in range(LAGS):
                rr, ii, mixed = sums[j], sums[LAGS + j], sums[2 * LAGS + j]
                cf[first + j, 0, at, :] = (mixed - rr - ii) * factor
                cf[first + j, 1, at, :] = (ii - rr) * factor
        return carry

    lax.fori_loop(0, rows // 8, one_slab, 0)


def kernel(
    n, ns, lesser, greater, diag_hbm, upper_hbm, out,
    diag, upper, gv, ht, lx, hx, lf, hf, cf, cx, polar, side, uprev, wside, total,
    lxb, hxb, lfb, hfb, cxb, partial,
    local_sem, send_sem, recv_l, recv_h, recv_p, side_send, side_recv, u_send, u_recv, half_send, half_recv,
):
    me = lax.axis_index("energy")
    row = lax.axis_index("space")
    chunks, _, k, _, rows, _ = lx.shape
    energies = n * k
    has_next = row < ns - 1
    has_prev = row > 0
    peers = n // 2
    half, member = me // peers, lax.rem(me, peers)
    own_energies = peers * k
    bands = lxb.shape[0]
    brows = bands * rows
    upper_half, lower_half = half == 1, half == 0

    barrier = pltpu.get_barrier_semaphore()

    def greet(step, carry):
        pl.semaphore_signal(
            barrier, inc=1, device_id=to_energy(lax.rem(me + step, n)), device_id_type=MESH
        )
        return carry

    lax.fori_loop(1, n, greet, 0)

    @pl.when(has_next)
    def _():
        pl.semaphore_signal(barrier, inc=1, device_id={"space": row + 1}, device_id_type=MESH)

    @pl.when(has_prev)
    def _():
        pl.semaphore_signal(barrier, inc=1, device_id={"space": row - 1}, device_id_type=MESH)

    load = pltpu.make_async_copy(greater.at[:, 0], gv, local_sem.at[0])
    load.start()
    load_upper = pltpu.make_async_copy(upper_hbm, upper, local_sem.at[1])
    load_upper.start()
    load_diag = pltpu.make_async_copy(diag_hbm, diag, local_sem.at[2])
    load_diag.start()
    load.wait()
    for e in range(k):
        for part_at in range(2):
            ht[e, part_at] = gv[e, part_at].T

    zeros = jnp.zeros((lf.shape[1] - energies,) + lf.shape[2:], jnp.float32)
    for q in range(3):
        lf[q, pl.ds(energies, lf.shape[1] - energies)] = zeros
    lfb[...] = jnp.zeros(lfb.shape, jnp.float32)

    pl.semaphore_wait(
        barrier, n - 1 + has_next.astype(jnp.int32) + has_prev.astype(jnp.int32)
    )

    def scatter(source, held, c, kind, recv):
        cols = pl.ds(c * LANES, LANES)

        def part(dest):
            return source.at[:, :, pl.ds(pl.multiple_of(dest * rows, rows), rows), cols]

        def push(step, carry):
            dest = lax.rem(me + step, n)
            pltpu.make_async_remote_copy(
                src_ref=part(dest), dst_ref=held.at[c, me], send_sem=send_sem.at[kind],
                recv_sem=recv.at[c], device_id=to_energy(dest), device_id_type=MESH,
            ).start()
            return carry

        lax.fori_loop(1, n, push, 0)
        pltpu.make_async_copy(part(me), held.at[c, me], recv.at[c]).start()

    u_copy = pltpu.make_async_remote_copy(
        src_ref=upper_hbm.at[0], dst_ref=uprev, send_sem=u_send, recv_sem=u_recv,
        device_id={"space": lax.rem(row + 1, ns)}, device_id_type=MESH,
    )

    @pl.when(has_next)
    def _():
        u_copy.start()

    def spread(pick, land, at_half, begin, kind, turn):
        def push(step, carry):
            peer = lax.rem(member + step, peers)
            dest = at_half * peers + peer
            pltpu.make_async_remote_copy(
                src_ref=pick(dest, peer), dst_ref=land(me, member), send_sem=half_send.at[kind],
                recv_sem=half_recv.at[kind, turn], device_id=to_energy(dest), device_id_type=MESH,
            ).start()
            return carry

        lax.fori_loop(begin, peers, push, 0)
        if begin:
            pltpu.make_async_copy(pick(me, member), land(me, member), half_recv.at[kind, turn]).start()

    def band_rows(peer, j):
        return pl.ds(pl.multiple_of(peer * brows + j * rows, rows), rows)

    def band(source, j):
        return lambda dest, peer: source.at[:, :, band_rows(peer, j), pl.ds(0, LANES)]

    def slot(buffer, j):
        return lambda at, peer: buffer.at[j, at]

    @pl.when(lower_half)
    def _():
        for j in range(bands):
            spread(band(ht, j), slot(hxb, j), 1, 0, 2, j)

    @pl.when(upper_half)
    def _():
        for j in range(bands):
            spread(band(lesser.at[:, 0], j), slot(lxb, j), half, 1, 0, j)
            spread(band(ht, j), slot(hxb, j), half, 1, 1, j)
    for c in range(1, chunks):
        scatter(lesser.at[:, 0], lx, c, 0, recv_l)
        scatter(ht, hx, c, 1, recv_h)

    @pl.when(lower_half)
    def _():
        for j in range(bands):
            spread(band(lesser.at[:, 0], j), slot(lxb, j), half, 1, 0, j)
            spread(band(ht, j), slot(hxb, j), half, 1, 1, j)

    load_upper.wait()
    load_diag.wait()
    wside[0] = upper[0]

    @pl.when(has_prev)
    def _():
        u_copy.wait_recv()
        wside[1] = uprev[...].T

    def arrived(buffer, kind, turn):
        pltpu.make_async_copy(buffer, buffer, half_recv.at[kind, turn]).wait()

    some = pl.ds(0, peers)
    own = pl.ds(half * peers, peers)
    short = (own_energies, rows, LANES)

    def half_bounds(first):
        begin = max(0, (own_energies - first - (LAGS + STEPS - 2)) // STEPS)
        low_end, high_end = max(0, own_energies - first) // STEPS, (energies - first) // STEPS
        return half * begin, low_end + half * (high_end - low_end)

    def landing(buffer, j):
        return lambda at, peer: buffer.at[:, :, band_rows(peer, j), :]

    for j in range(bands):
        own_at = pl.ds(half * own_energies, own_energies)
        arrived(lxb.at[j, some], 0, j)
        widen_into(lfb, own_at, lxb[j, own, :, 0].reshape(short), lxb[j, own, :, 1].reshape(short))
        arrived(hxb.at[j, some], 1, j)
        widen_into(hfb, own_at, hxb[j, own, :, 0].reshape(short), hxb[j, own, :, 1].reshape(short))

        @pl.when(upper_half)
        def _():
            arrived(hxb.at[j, some], 2, j)
            re, im = hxb[j, some, :, 0].reshape(short), hxb[j, some, :, 1].reshape(short)
            widen_into(hfb, pl.ds(0, own_energies), re, im)

        correlate_into(cf, lfb, hfb, half_bounds)
        cxb[j] = cf[...].astype(jnp.bfloat16).reshape(cxb.shape[1:])

        @pl.when(upper_half)
        def _():
            spread(lambda dest, peer: cxb.at[j, dest], landing(partial, j), 0, 0, 4, 0)

        spread(lambda dest, peer: cxb.at[j, dest], landing(polar.at[0], j), half, 1, 3, 0)

    def one_chunk(c, carry):
        pltpu.make_async_copy(lx.at[c], lx.at[c], recv_l.at[c]).wait()
        pltpu.make_async_copy(hx.at[c], hx.at[c], recv_h.at[c]).wait()
        flat = (energies, rows, LANES)
        for held, wide in ((lx, lf), (hx, hf)):
            widen_into(wide, pl.ds(0, energies), held[c, :, :, 0].reshape(flat), held[c, :, :, 1].reshape(flat))
        correlate_into(cf, lf, hf, lambda first: (0, (energies - first) // STEPS))
        cx[c] = cf[...].astype(jnp.bfloat16).reshape(cx.shape[1:])
        mine = pl.ds(pl.multiple_of(me * rows, rows), rows)

        def push(step, carry_in):
            dest = lax.rem(me + step, n)
            pltpu.make_async_remote_copy(
                src_ref=cx.at[c, dest], dst_ref=polar.at[c, :, :, mine, :],
                send_sem=send_sem.at[2], recv_sem=recv_p.at[c],
                device_id=to_energy(dest), device_id_type=MESH,
            ).start()
            return carry_in

        lax.fori_loop(1, n, push, 0)
        pltpu.make_async_copy(cx.at[c, me], polar.at[c, :, :, mine, :], recv_p.at[c]).start()
        return carry

    lax.fori_loop(1, chunks, one_chunk, 0)

    def screen(block, coupler, slot, c, begin):
        right = coupler[:, c * LANES:(c + 1) * LANES]
        for e in range(k):
            pair = jnp.concatenate([block[slot, e, 0], block[slot, e, 1]], axis=1)
            left = jnp.dot(coupler, pair, preferred_element_type=jnp.float32).astype(jnp.bfloat16)
            for part_at in range(2):
                term = lax.dot_general(
                    left[:, part_at * LANES:(part_at + 1) * LANES], right,
                    (((1,), (1,)), ((), ())), preferred_element_type=jnp.float32,
                )
                if begin:
                    total[e, part_at] = term
                else:
                    total[e, part_at] += term

    def forward(c, slot, to):
        return pltpu.make_async_remote_copy(
            src_ref=polar.at[c], dst_ref=side.at[slot, c], send_sem=side_send.at[slot, c],
            recv_sem=side_recv.at[slot, c], device_id={"space": to}, device_id_type=MESH,
        )

    up, down = lax.rem(row + 1, ns), lax.rem(row + ns - 1, ns)
    for c in range(chunks):
        if c:
            pltpu.make_async_copy(polar.at[c], polar.at[c], recv_p.at[c]).wait()
        else:
            arrived(polar.at[0], 3, 0)

            @pl.when(lower_half)
            def _():
                arrived(partial, 4, 0)
                both = polar[0].astype(jnp.float32) + partial[...].astype(jnp.float32)
                polar[0] = both.astype(jnp.bfloat16)

        @pl.when(has_prev)
        def _():
            forward(c, 0, down).start()

        @pl.when(has_next)
        def _():
            forward(c, 1, up).start()

        screen(polar, diag[0], c, c, c == 0)

        @pl.when(has_next)
        def _():
            forward(c, 0, down).wait_recv()
            screen(side.at[0], wside[0], c, c, False)

        @pl.when(has_prev)
        def _():
            forward(c, 1, up).wait_recv()
            screen(side.at[1], wside[1], c, c, False)

    out[:, 0] = total[...].astype(jnp.bfloat16)

    for c in range(chunks):
        @pl.when(has_prev)
        def _():
            forward(c, 0, down).wait_send()

        @pl.when(has_next)
        def _():
            forward(c, 1, up).wait_send()

    @pl.when(has_next)
    def _():
        u_copy.wait_send()

    for kind in range(3):
        sent = lx.at[pl.ds(1, chunks - 1), pl.ds(0, n - 1)]
        pltpu.make_async_copy(sent, sent, send_sem.at[kind]).wait()

    def left_here(count, kind):
        sent = lxb.at[:, pl.ds(0, count)]
        pltpu.make_async_copy(sent, sent, half_send.at[kind]).wait()

    for kind in (0, 1, 3):
        left_here(peers - 1, kind)

    @pl.when(lower_half)
    def _():
        left_here(peers, 2)

    @pl.when(upper_half)
    def _():
        left_here(peers, 4)


def fused(n, ns, lesser, greater, diag, upper):
    k, _, _, size, _ = lesser.shape
    rows, chunks, energies = size // n, size // LANES, n * k
    bf, f32 = jnp.bfloat16, jnp.float32
    whole = (k, 2, size, size)
    padded = energies + LAGS + STEPS
    dma = pltpu.SemaphoreType.DMA
    vmem = pl.BlockSpec(memory_space=pltpu.VMEM)
    hbm = pl.BlockSpec(memory_space=pltpu.HBM)
    return pl.pallas_call(
        functools.partial(kernel, n, ns),
        out_shape=jax.ShapeDtypeStruct(lesser.shape, bf),
        in_specs=[hbm] * 4,
        out_specs=vmem,
        scratch_shapes=[
            pltpu.VMEM(diag.shape, bf),
            pltpu.VMEM(upper.shape, bf),
            pltpu.VMEM(whole, bf),
            pltpu.VMEM(whole, bf),
            pltpu.VMEM((chunks, n, k, 2, rows, LANES), bf),
            pltpu.VMEM((chunks, n, k, 2, rows, LANES), bf),
            pltpu.VMEM((3, padded, rows, LANES), f32),
            pltpu.VMEM((3, energies, rows, LANES), f32),
            pltpu.VMEM((energies, 2, rows, LANES), f32),
            pltpu.VMEM((chunks, n, k, 2, rows, LANES), bf),
            pltpu.VMEM((chunks, k, 2, size, LANES), bf),
            pltpu.VMEM((2, chunks, k, 2, size, LANES), bf),
            pltpu.VMEM((size, size), bf),
            pltpu.VMEM((2, size, size), bf),
            pltpu.VMEM(whole, f32),
            pltpu.VMEM((2, n, k, 2, rows, LANES), bf),
            pltpu.VMEM((2, n, k, 2, rows, LANES), bf),
            pltpu.VMEM((3, padded, rows, LANES), f32),
            pltpu.VMEM((3, energies, rows, LANES), f32),
            pltpu.VMEM((2, n, k, 2, rows, LANES), bf),
            pltpu.VMEM((k, 2, size, LANES), bf),
            dma((3,)), dma((3,)), dma((chunks,)), dma((chunks,)), dma((chunks,)),
            dma((2, chunks)), dma((2, chunks)), dma, dma,
            dma((5,)), dma((5, 2)),
        ],
        compiler_params=pltpu.CompilerParams(
            collective_id=0, has_side_effects=True, vmem_limit_bytes=40 << 20
        ),
    )(*(pltpu.with_memory_space_constraint(x, pltpu.HBM) for x in (lesser, greater, diag, upper)))


def fits(n, ns, size, energies):
    banded = n % 2 == 0 and size % n == 0 and (size // n) % 16 == 0 and size % LANES == 0
    return banded and size > LANES and energies % (2 * LAGS) == 0 and ns > 1


def either(n, ns, lesser, greater, diag, upper):
    if fits(n, ns, lesser.shape[3], n * lesser.shape[0]):
        return fused(n, ns, lesser, greater, diag, upper)
    return per_device(lesser, greater, diag, upper)


def solution(mesh):
    placed = (
        P("energy", "space", None, None, None),
        P("energy", "space", None, None, None),
        P("space", None, None),
        P("space", None, None),
    )
    return jax.shard_map(
        functools.partial(either, mesh.shape["energy"], mesh.shape["space"]),
        mesh=mesh,
        in_specs=placed,
        out_specs=P("energy", "space", None, None, None),
        check_vma=False,
    )
```
